32 devices in a mesh: gx: 2 (over x), yz: 16 (over z, y, core).
Axes of the slice: x: 2, y: 2, z: 4, core: 2. Of those that a mesh axis runs over, the one named last changes fastest.
Arguments:
- tensor: float32 [4, 512, 32, 32], P(None, 'gx', 'yz'), may hold values from -40 to 40
- start_basis: float32 [96, 512], replicated, may hold values from -6 to 6
Outputs:
- core_tensor: float32 [32, 32, 384], P(('gx', 'yz'))
- factor: float32 [96, 512], replicated
The draws below stay inside these ranges and needn't reach their ends.
All inputs are finite; a program needn't handle non-finite values.
Results may differ from the reference program's by a relative error of at most 0.00012.
Values sent between devices are 32-bit elements; how exact they have to be, the bound alone decides.
A program may use at most 64 MiB of HBM per device.

```python
import math
import jax
import jax.numpy as jnp
from jax import lax

S = 4
NX = 512
K = 96
NY = 32
NZ = 32


def draw_tensor(key, part):
    keys_all = jax.random.split(jax.random.fold_in(key, 17), 5)
    full_shape = (S, NX, NY, NZ)
    row_scale = 0.2 * jnp.exp(jax.random.uniform(keys_all[0], (NX,), jnp.float32, 0.0, math.log(2.5)))
    line_scale = 0.3 * jnp.exp(jax.random.uniform(keys_all[1], (NY,), jnp.float32, 0.0, math.log(10.0)))
    noise = jnp.clip(jax.random.normal(keys_all[2], full_shape, jnp.float32), -5.0, 5.0)
    components = 4
    load_rows = jax.random.uniform(keys_all[3], (components, NX), jnp.float32, -0.15, 0.15)
    factors = jnp.clip(jax.random.normal(keys_all[4], (components, S, NY, NZ), jnp.float32), -4.0, 4.0)
    shared = jnp.zeros(full_shape, jnp.float32)
    for component in range(components):
        shared = shared + load_rows[component][None, :, None, None] * factors[component][:, None, :, :]
    return row_scale[None, :, None, None] * line_scale[None, None, :, None] * (noise + shared)


def bell_draw(stream_key, extent, spread, limit, held_as=jnp.bfloat16):
    return jnp.clip(spread * jax.random.normal(stream_key, extent, jnp.float32), -limit, limit).astype(held_as)


def setup_inputs(seed: int = 0) -> dict:
    streams_of = jax.random.split(jax.random.key(seed), 3)
    return {
        "tensor": draw_tensor(jax.random.fold_in(streams_of[2], 71), 0),
        "start_basis": bell_draw(streams_of[1], (K, NX), 1.0, 6.0, jnp.float32),
    }


def orthonormal(image_rows):
    small_gram = jnp.dot(image_rows, image_rows.T, precision=lax.Precision.HIGHEST)
    lower_factor = jnp.linalg.cholesky(small_gram)
    return lax.linalg.triangular_solve(lower_factor, image_rows, left_side=True, lower=True)

def reference(tensor, start_basis):
    cell_count = S * NY * NZ

    def accumulate(line_index, gram_matrix):
        plane = lax.dynamic_slice_in_dim(tensor, line_index, 1, 2)
        return gram_matrix + lax.dot_general(plane, plane, (((0, 2, 3), (0, 2, 3)), ((), ())), precision=lax.Precision.HIGHEST)
    gram_matrix = lax.fori_loop(0, NY, accumulate, jnp.zeros((NX, NX), jnp.float32)) / cell_count
    basis = start_basis
    for repeat in range(2):
        basis = orthonormal(jnp.dot(basis, gram_matrix, precision=lax.Precision.HIGHEST))
    core_tensor = jnp.einsum('kx,sxyz->zysk', basis, tensor, precision=lax.Precision.HIGHEST)
    return (core_tensor.reshape(NZ, NY, S * K), basis)
```

```python
import functools

import jax
import jax.numpy as jnp
from jax import lax
from jax.experimental import pallas as pl
from jax.experimental.pallas import tpu as pltpu
from jax.sharding import PartitionSpec as P

HIGHEST = lax.Precision.HIGHEST
MESH = pl.DeviceIdType.MESH
LANES = 128
SUBLANES = 8


def mm(a, b):
    return lax.dot_general(
        a, b, (((1,), (0,)), ((), ())), precision=HIGHEST, preferred_element_type=jnp.float32
    )


def mm_nt(a, b):
    return lax.dot_general(
        a, b, (((1,), (1,)), ((), ())), precision=HIGHEST, preferred_element_type=jnp.float32
    )


def inverse_cholesky(gram, panel=SUBLANES):
    rank = gram.shape[0]
    wide = -(-rank // LANES) * LANES
    row_id = lax.broadcasted_iota(jnp.int32, (rank, wide), 0)
    lane_id = lax.broadcasted_iota(jnp.int32, (rank, wide), 1)
    left = jnp.concatenate([gram, jnp.zeros((rank, wide - rank), jnp.float32)], axis=1) if wide > rank else gram
    right = jnp.where(row_id == lane_id, 1.0, 0.0).astype(jnp.float32)
    done_right = []
    for base in range(0, rank, SUBLANES):
        rows = rank - base
        local_row = lax.broadcasted_iota(jnp.int32, (rows, wide), 0)
        pivots = jnp.zeros((SUBLANES, wide), jnp.float32)
        for first in range(0, SUBLANES, panel):
            spread = [
                jnp.broadcast_to(left[:, base + step : base + step + 1], (rows, wide))
                for step in range(first, first + panel)
            ]
            for step in range(first, first + panel):
                column = spread[step - first]
                pivot = column[step : step + 1]
                pivots = jnp.where(local_row[:SUBLANES] == step, jnp.broadcast_to(pivot, (SUBLANES, wide)), pivots)
                factor = jnp.where(local_row > step, column * (1.0 / pivot), 0.0)
                for other in range(step + 1, first + panel):
                    spread[other - first] = spread[other - first] - factor * spread[other - first][step : step + 1]
                left = left - factor * left[step : step + 1]
                right = right - factor * right[step : step + 1]
        done_right.append(right[:SUBLANES] / jnp.sqrt(pivots))
        left, right = left[SUBLANES:], right[SUBLANES:]
    return jnp.concatenate(done_right, axis=0)[:, :rank]


def kernel(
    shape,
    x_hbm,
    start_hbm,
    core_ref,
    factor_ref,
    xf,
    start,
    stage,
    parts,
    sums,
    core_out,
    local_sem,
    x_send,
    x_recv,
    relay_send,
    relay_recv,
    sum_send,
    sum_recv,
    all_send,
    all_recv,
    pair_send,
    pair_recv,
    core_send,
    core_recv,
):
    n_gx, n_yz, cell_count = shape
    n = n_gx * n_yz
    my_x, my_yz = lax.axis_index("gx"), lax.axis_index("yz")
    me = my_x * n_yz + my_yz
    core = lax.rem(my_yz, 2)
    mine = lax.div(me, 2)
    other_x = 1 - my_x
    _, _, species, lines, cells_z, width = xf.shape
    half = start.shape[1]
    rank = 2 * half
    owners, rows = stage.shape[1:3]
    per_column = half // rows
    held_cells = species * lines * cells_z
    flips = [1 - 2 * lax.rem(lax.div(me, 1 << bit), 2) for bit in range(n.bit_length() - 1)]
    peers = range(n - 2, 0, -2)

    def place(flat):
        return {"gx": lax.div(flat, n_yz), "yz": lax.rem(flat, n_yz)}

    def partner(k):
        return me + sum((1 << bit) * flip for bit, flip in enumerate(flips) if k >> bit & 1)

    def remote(src, dst, send, recv, k):
        return pltpu.make_async_remote_copy(
            src_ref=src, dst_ref=dst, send_sem=send, recv_sem=recv, device_id=place(partner(k)), device_id_type=MESH
        )

    barrier = pltpu.get_barrier_semaphore()
    across = n_yz
    for k in [across, 1, *(k for k in range(n - 1, 0, -1) if k not in (across, 1))]:
        pl.semaphore_signal(barrier, inc=1, device_id=place(partner(k)), device_id_type=MESH)

    kept = pl.ds(my_x * lines, lines)
    given = pl.ds(other_x * lines, lines)
    own_copy = pltpu.make_async_copy(x_hbm.at[:, kept], xf.at[my_x, 0], local_sem.at[0])
    own_copy.start()
    mine_rows = pl.ds(pl.multiple_of(core * half, SUBLANES), half)
    start_copies = [
        pltpu.make_async_copy(
            start_hbm.at[mine_rows, part * width : (part + 1) * width], start.at[part], local_sem.at[1 + part]
        )
        for part in range(n_gx)
    ]
    for copy in start_copies:
        copy.start()

    with jax.named_scope("s_barrier"):
        pl.semaphore_wait(barrier, n - 1)

    x_copies = [
        remote(x_hbm.at[s, given], xf.at[my_x, 0, s], x_send.at[s], x_recv.at[s], across) for s in range(species)
    ]
    x_arrivals = [
        remote(x_hbm.at[s, given], xf.at[other_x, 0, s], x_send.at[s], x_recv.at[s], across) for s in range(species)
    ]
    kept_copy = remote(x_hbm.at[:, kept], xf.at[my_x, 1], relay_send.at[species], relay_recv.at[species], 1)
    relays = [
        remote(xf.at[other_x, 0, s], xf.at[other_x, 1, s], relay_send.at[s], relay_recv.at[s], 1)
        for s in range(species)
    ]

    def cells(part, side):
        return xf[part, side].reshape(held_cells, width)

    with jax.named_scope("s_xex"):
        for copy in x_copies:
            copy.start()
        kept_copy.start()
        own_copy.wait()
        for copy in start_copies:
            copy.wait()
        kept_copy.wait_recv()
        projected = [mm_nt(start[my_x], cells(my_x, side)) for side in range(2)]
        for arrival, relay in zip(x_arrivals, relays):
            arrival.wait_recv()
            relay.start()
        projected[0] = projected[0] + mm_nt(start[other_x], cells(other_x, 0))
        for relay in relays:
            relay.wait_recv()
        projected[1] = projected[1] + mm_nt(start[other_x], cells(other_x, 1))

    def image_of(projected):
        projected = [term * (1.0 / cell_count) for term in projected]
        columns = [sum(mm(projected[side], cells(part, side)) for side in range(2)) for part in range(n_gx)]
        return jnp.concatenate(columns, axis=1)

    def sum_copy(turn, k):
        return remote(
            stage.at[turn, lax.div(partner(k), 2)],
            parts.at[turn, k // 2 - 1],
            sum_send.at[turn, k // 2 - 1],
            sum_recv.at[turn, k // 2 - 1],
            k,
        )

    def all_copy(turn, k):
        return remote(
            sums.at[turn, core, mine],
            sums.at[turn, core, mine],
            all_send.at[turn, k // 2 - 1],
            all_recv.at[turn, k // 2 - 1],
            k,
        )

    def all_arrival(turn, k):
        return remote(
            sums.at[turn, core, mine],
            sums.at[turn, core, lax.div(partner(k), 2)],
            all_send.at[turn, k // 2 - 1],
            all_recv.at[turn, k // 2 - 1],
            k,
        )

    def pair_copy(turn, k):
        block = lax.div(partner(k), 2)
        return remote(
            sums.at[turn, core, block],
            sums.at[turn, core, block],
            pair_send.at[turn, k // 2],
            pair_recv.at[turn, k // 2],
            1,
        )

    def pair_arrival(turn, k):
        block = lax.div(partner(k), 2)
        return remote(
            sums.at[turn, core, block],
            sums.at[turn, 1 - core, block],
            pair_send.at[turn, k // 2],
            pair_recv.at[turn, k // 2],
            1,
        )

    def spread(turn, image):
        for owner in range(owners):
            column, block = owner // per_column, owner % per_column
            stage[turn, owner] = image[block * rows : (block + 1) * rows, column * LANES : (column + 1) * LANES]
        for k in peers:
            sum_copy(turn, k).start()

    def total(turn):
        terms = [stage[turn, mine]]
        for k in reversed(peers):
            sum_copy(turn, k).wait_recv()
            terms.append(parts[turn, k // 2 - 1])
        while len(terms) > 1:
            terms = [a + b for a, b in zip(terms[::2], terms[1::2])] + ([terms[-1]] if len(terms) % 2 else [])
        sums[turn, core, mine] = terms[0]
        for k in peers:
            all_copy(turn, k).start()
        pair_copy(turn, 0).start()

    def gathered(turn, side):
        blocks = [sums[turn, side, owner] for owner in range(owners)]
        columns = [jnp.concatenate(blocks[at : at + per_column], axis=0) for at in range(0, owners, per_column)]
        return jnp.concatenate(columns, axis=1)

    def collect(turn):
        for k in reversed(peers):
            all_arrival(turn, k).wait_recv()
            pair_copy(turn, k).start()

    def whole(turn):
        for k in [0, *reversed(peers)]:
            pair_arrival(turn, k).wait_recv()
        return jnp.concatenate([gathered(turn, side) for side in range(2)], axis=0)

    with jax.named_scope("s_img0"):
        spread(0, image_of(projected))
    with jax.named_scope("s_rs0"):
        total(0)
    with jax.named_scope("s_ag0"):
        collect(0)
    with jax.named_scope("s_img1"):
        image = gathered(0, core)
        projected = []
        for side in range(2):
            terms = [
                mm_nt(image[:, part * width : (part + 1) * width], cells(part, side)) for part in range(n_gx)
            ]
            projected.append(sum(terms[1:], terms[0]))
        spread(1, image_of(projected))
    with jax.named_scope("s_rs1"):
        total(1)
    with jax.named_scope("s_chol0"):
        image = whole(0)
        inverse = inverse_cholesky(mm_nt(image, image))
    with jax.named_scope("s_ag1"):
        collect(1)
    with jax.named_scope("s_pair1"):
        image = whole(1)
    with jax.named_scope("s_chol1"):
        image = mm(inverse, image)
        inverse = inverse_cholesky(mm_nt(image, image))
        raw = None
        for part in range(n_gx):
            term = mm_nt(cells(part, 0), image[:, part * width : (part + 1) * width])
            raw = term if raw is None else raw + term
        truncated = mm_nt(raw, inverse)

    share = cells_z // n
    for s in range(species):
        for line in range(lines):
            at = (s * lines + line) * cells_z
            core_out[:, line, s * rank : (s + 1) * rank] = truncated[at : at + cells_z]

    spot = my_yz * n_gx + my_x

    def core_copy(k):
        peer = partner(k)
        return remote(
            core_out.at[pl.ds(peer * share, share)], core_ref.at[spot], core_send.at[k - 1], core_recv.at[k - 1], k
        )

    def core_arrival(k):
        source = partner(k)
        spot_of = lax.rem(source, n_yz) * n_gx + lax.div(source, n_yz)
        return remote(
            core_out.at[pl.ds(source * share, share)],
            core_ref.at[spot_of],
            core_send.at[k - 1],
            core_recv.at[k - 1],
            k,
        )

    everyone = range(n - 1, 0, -1)
    with jax.named_scope("s_a2astart"):
        for k in everyone:
            core_copy(k).start()
    with jax.named_scope("s_factor"):
        core_ref[spot] = core_out[pl.ds(me * share, share)]
        factor_ref[...] = mm(inverse, image)
    with jax.named_scope("s_drain"):
        for copy in x_copies:
            copy.wait_send()
        for copy in [*relays, kept_copy]:
            copy.wait_send()
        for turn in range(2):
            for k in peers:
                sum_copy(turn, k).wait_send()
                all_copy(turn, k).wait_send()
                pair_copy(turn, k).wait_send()
            pair_copy(turn, 0).wait_send()
    with jax.named_scope("s_a2await"):
        for k in everyone:
            core_arrival(k).wait()


def finish(core_in, factor_in, core_hbm, factor_hbm, core_buf, sem):
    lines = core_in.shape[2]
    factor_copy = pltpu.make_async_copy(factor_in, factor_hbm, sem.at[0])
    factor_copy.start()
    for spot in range(core_in.shape[0]):
        core_buf[:, spot * lines : (spot + 1) * lines] = core_in[spot]
    core_copy = pltpu.make_async_copy(core_buf, core_hbm, sem.at[1])
    core_copy.start()
    factor_copy.wait()
    core_copy.wait()


def kernel_program(tensor, start_basis, n_gx, n_yz, rows):
    n = n_gx * n_yz
    species, width, lines_held, cells_z = tensor.shape
    rank, total = start_basis.shape
    half = rank // 2
    lines = lines_held // n_gx
    cell_count = species * lines_held * n_yz * cells_z
    share = cells_z // n
    out = species * rank
    owners = n // 2
    dma = pltpu.SemaphoreType.DMA
    core, factor = pl.pallas_call(
        functools.partial(kernel, (n_gx, n_yz, cell_count)),
        out_shape=(
            pltpu.VMEM((n, share, lines, out), jnp.float32),
            pltpu.VMEM((rank, total), jnp.float32),
        ),
        in_specs=[pl.BlockSpec(memory_space=pltpu.HBM)] * 2,
        out_specs=(pl.BlockSpec(memory_space=pltpu.VMEM),) * 2,
        scratch_shapes=[
            pltpu.VMEM((n_gx, 2, species, lines, cells_z, width), jnp.float32),
            pltpu.VMEM((n_gx, half, width), jnp.float32),
            pltpu.VMEM((2, owners, rows, LANES), jnp.float32),
            pltpu.VMEM((2, owners - 1, rows, LANES), jnp.float32),
            pltpu.VMEM((2, 2, owners, rows, LANES), jnp.float32),
            pltpu.VMEM((cells_z, lines, out), jnp.float32),
            dma((1 + n_gx,)),
            dma((species,)),
            dma((species,)),
            dma((species + 1,)),
            dma((species + 1,)),
            dma((2, owners - 1)),
            dma((2, owners - 1)),
            dma((2, owners - 1)),
            dma((2, owners - 1)),
            dma((2, owners)),
            dma((2, owners)),
            dma((n - 1,)),
            dma((n - 1,)),
        ],
        compiler_params=pltpu.CompilerParams(collective_id=0, has_side_effects=True),
    )(tensor.transpose(0, 2, 3, 1), start_basis)
    return pl.pallas_call(
        finish,
        out_shape=(
            jax.ShapeDtypeStruct((share, n * lines, out), jnp.float32),
            jax.ShapeDtypeStruct((rank, total), jnp.float32),
        ),
        in_specs=[pl.BlockSpec(memory_space=pltpu.VMEM)] * 2,
        out_specs=(pl.BlockSpec(memory_space=pltpu.HBM),) * 2,
        scratch_shapes=[pltpu.VMEM((share, n * lines, out), jnp.float32), dma((2,))],
        compiler_params=pltpu.CompilerParams(vmem_limit_bytes=4 << 20),
    )(core, factor)


def orthonormal(image_rows):
    small_gram = jnp.dot(image_rows, image_rows.T, precision=HIGHEST)
    lower_factor = jnp.linalg.cholesky(small_gram)
    return lax.linalg.triangular_solve(lower_factor, image_rows, left_side=True, lower=True)


def collective_program(tensor, start_basis):
    regrouped = lax.all_to_all(tensor, "gx", split_axis=2, concat_axis=1, tiled=True)
    species, _, lines, cells_z = regrouped.shape
    cell_count = species * lines * lax.axis_size("gx") * lax.axis_size("yz") * cells_z
    gram_matrix = lax.dot_general(
        regrouped, regrouped, (((0, 2, 3), (0, 2, 3)), ((), ())), precision=HIGHEST
    )
    gram_matrix = lax.psum(gram_matrix, ("gx", "yz")) / cell_count
    basis = start_basis
    for _ in range(2):
        basis = orthonormal(jnp.dot(basis, gram_matrix, precision=HIGHEST))
    core_local = jnp.einsum("kx,sxyz->zysk", basis, regrouped, precision=HIGHEST)
    core_local = core_local.reshape(cells_z, lines, species * basis.shape[0])
    core_tensor = lax.all_to_all(
        lax.all_to_all(core_local, "gx", split_axis=0, concat_axis=1, tiled=True),
        "yz",
        split_axis=0,
        concat_axis=1,
        tiled=True,
    )
    return core_tensor, basis


def solution(mesh):
    n_gx, n_yz = mesh.shape["gx"], mesh.shape["yz"]
    n = n_gx * n_yz

    def local(tensor, start_basis):
        species, width, lines_held, cells_z = tensor.shape
        rank, total = start_basis.shape
        half, owners = rank // 2, n // 2
        fits = n_gx == 2 and n_yz % 2 == 0 and n & (n - 1) == 0 and rank % (2 * SUBLANES) == 0
        fits = fits and width % LANES == 0 and lines_held % n_gx == 0 and cells_z % max(n, SUBLANES) == 0
        fits = fits and species * width * lines_held * cells_z <= 1 << 19
        rows, left_over = divmod(half * (total // LANES), owners)
        if fits and left_over == 0 and rows and half % rows == 0:
            return kernel_program(tensor, start_basis, n_gx, n_yz, rows)
        return collective_program(tensor, start_basis)

    return jax.shard_map(
        local,
        mesh=mesh,
        in_specs=(P(None, "gx", "yz", None), P()),
        out_specs=(P(("gx", "yz"), None, None), P()),
        check_vma=False,
    )
```

```python
import functools

import jax
import jax.numpy as jnp
from jax import lax
from jax.experimental import pallas as pl
from jax.experimental.pallas import tpu as pltpu
from jax.sharding import PartitionSpec as P

HIGHEST = lax.Precision.HIGHEST
MESH = pl.DeviceIdType.MESH
LANES = 128
SUBLANES = 8


def mm(a, b):
    return lax.dot_general(
        a, b, (((1,), (0,)), ((), ())), precision=HIGHEST, preferred_element_type=jnp.float32
    )


def mm_nt(a, b):
    return lax.dot_general(
        a, b, (((1,), (1,)), ((), ())), precision=HIGHEST, preferred_element_type=jnp.float32
    )


def inverse_cholesky(gram, panel=SUBLANES):
    rank = gram.shape[0]
    wide = -(-rank // LANES) * LANES
    row_id = lax.broadcasted_iota(jnp.int32, (rank, wide), 0)
    lane_id = lax.broadcasted_iota(jnp.int32, (rank, wide), 1)
    left = jnp.concatenate([gram, jnp.zeros((rank, wide - rank), jnp.float32)], axis=1) if wide > rank else gram
    right = jnp.where(row_id == lane_id, 1.0, 0.0).astype(jnp.float32)
    done_right = []
    for base in range(0, rank, SUBLANES):
        rows = rank - base
        local_row = lax.broadcasted_iota(jnp.int32, (rows, wide), 0)
        pivots = jnp.zeros((SUBLANES, wide), jnp.float32)
        for first in range(0, SUBLANES, panel):
            spread = [
                jnp.broadcast_to(left[:, base + step : base + step + 1], (rows, wide))
                for step in range(first, first + panel)
            ]
            for step in range(first, first + panel):
                column = spread[step - first]
                pivot = column[step : step + 1]
                pivots = jnp.where(local_row[:SUBLANES] == step, jnp.broadcast_to(pivot, (SUBLANES, wide)), pivots)
                factor = jnp.where(local_row > step, column * (1.0 / pivot), 0.0)
                for other in range(step + 1, first + panel):
                    spread[other - first] = spread[other - first] - factor * spread[other - first][step : step + 1]
                left = left - factor * left[step : step + 1]
                right = right - factor * right[step : step + 1]
        done_right.append(right[:SUBLANES] / jnp.sqrt(pivots))
        left, right = left[SUBLANES:], right[SUBLANES:]
    return jnp.concatenate(done_right, axis=0)[:, :rank]


def kernel(
    shape,
    x_hbm,
    start_hbm,
    core_ref,
    factor_ref,
    xf,
    start,
    stage,
    parts,
    sums,
    core_out,
    local_sem,
    send_sem,
    x_recv,
    relay_recv,
    sum_recv,
    all_recv,
    pair_recv,
    core_recv,
):
    n_gx, n_yz, cell_count = shape
    n = n_gx * n_yz
    my_x, my_yz = lax.axis_index("gx"), lax.axis_index("yz")
    me = my_x * n_yz + my_yz
    core = lax.rem(my_yz, 2)
    mine = lax.div(me, 2)
    other_x = 1 - my_x
    _, _, species, lines, cells_z, width = xf.shape
    half = start.shape[1]
    rank = 2 * half
    owners, rows = stage.shape[1:3]
    per_column = half // rows
    held_cells = species * lines * cells_z
    flips = [1 - 2 * lax.rem(lax.div(me, 1 << bit), 2) for bit in range(n.bit_length() - 1)]
    peers = range(n - 2, 0, -2)

    def place(flat):
        return {"gx": lax.div(flat, n_yz), "yz": lax.rem(flat, n_yz)}

    def partner(k):
        return me + sum((1 << bit) * flip for bit, flip in enumerate(flips) if k >> bit & 1)

    def remote(src, dst, send, recv, k):
        return pltpu.make_async_remote_copy(
            src_ref=src,
            dst_ref=dst,
            send_sem=send_sem.at[send],
            recv_sem=recv,
            device_id=place(partner(k)),
            device_id_type=MESH,
        )

    def take(ref, sem):
        pltpu.make_async_copy(ref, ref, sem).wait()

    barrier = pltpu.get_barrier_semaphore()
    across = n_yz
    for k in [across, 1, *(k for k in range(n - 1, 0, -1) if k not in (across, 1))]:
        pl.semaphore_signal(barrier, inc=1, device_id=place(partner(k)), device_id_type=MESH)

    kept = pl.ds(my_x * lines, lines)
    given = pl.ds(other_x * lines, lines)
    own_copy = pltpu.make_async_copy(x_hbm.at[:, kept], xf.at[my_x, 0], local_sem.at[0])
    own_copy.start()
    mine_rows = pl.ds(pl.multiple_of(core * half, SUBLANES), half)
    for part in range(n_gx):
        pltpu.make_async_copy(
            start_hbm.at[mine_rows, part * width : (part + 1) * width], start.at[part], local_sem.at[1]
        ).start()

    with jax.named_scope("s_barrier"):
        pl.semaphore_wait(barrier, n - 1)

    x_copies = [remote(x_hbm.at[s, given], xf.at[my_x, 0, s], 0, x_recv.at[s], across) for s in range(species)]
    kept_copy = remote(x_hbm.at[:, kept], xf.at[my_x, 1], 1, relay_recv.at[0], 1)
    relays = [remote(xf.at[other_x, 0, s], xf.at[other_x, 1, s], 1, relay_recv.at[1], 1) for s in range(species)]

    def cells(part, side):
        return xf[part, side].reshape(held_cells, width)

    with jax.named_scope("s_xex"):
        for copy in x_copies:
            copy.start()
        kept_copy.start()
        own_copy.wait()
        take(start, local_sem.at[1])
        take(xf.at[my_x, 1], relay_recv.at[0])
        projected = [mm_nt(start[my_x], cells(my_x, side)) for side in range(2)]
        for s, relay in enumerate(relays):
            take(xf.at[other_x, 0, s], x_recv.at[s])
            relay.start()
        projected[0] = projected[0] + mm_nt(start[other_x], cells(other_x, 0))
        take(xf.at[other_x, 1], relay_recv.at[1])
        projected[1] = projected[1] + mm_nt(start[other_x], cells(other_x, 1))

    def image_of(projected):
        projected = [term * (1.0 / cell_count) for term in projected]
        columns = [sum(mm(projected[side], cells(part, side)) for side in range(2)) for part in range(n_gx)]
        return jnp.concatenate(columns, axis=1)

    def sum_copy(turn, k):
        block = lax.div(partner(k), 2)
        return remote(stage.at[turn, block], parts.at[turn, k // 2 - 1], 2 + turn, sum_recv.at[turn], k)

    def all_copy(turn, k):
        block = sums.at[turn, core, mine]
        return remote(block, block, 4 + turn, all_recv.at[k // 2 if turn else 0], k)

    def pair_copy(turn, k):
        block = sums.at[turn, core, lax.div(partner(k), 2)]
        return remote(block, block, 7, pair_recv.at[1], 1)

    def spread(turn, image):
        for owner in range(owners):
            column, block = owner // per_column, owner % per_column
            stage[turn, owner] = image[block * rows : (block + 1) * rows, column * LANES : (column + 1) * LANES]
        for k in peers:
            sum_copy(turn, k).start()

    def total(turn):
        take(parts.at[turn], sum_recv.at[turn])
        terms = [stage[turn, mine]] + [parts[turn, k // 2 - 1] for k in peers]
        while len(terms) > 1:
            terms = [a + b for a, b in zip(terms[::2], terms[1::2])] + ([terms[-1]] if len(terms) % 2 else [])
        sums[turn, core, mine] = terms[0]
        for k in peers:
            all_copy(turn, k).start()

    def gathered(turn, side):
        blocks = [sums[turn, side, owner] for owner in range(owners)]
        columns = [jnp.concatenate(blocks[at : at + per_column], axis=0) for at in range(0, owners, per_column)]
        return jnp.concatenate(columns, axis=1)

    held = pl.ds(0, owners - 1)

    def whole(turn):
        take(sums.at[turn, 1 - core], pair_recv.at[turn])
        return jnp.concatenate([gathered(turn, side) for side in range(2)], axis=0)

    with jax.named_scope("s_img0"):
        spread(0, image_of(projected))
    with jax.named_scope("s_rs0"):
        total(0)
    with jax.named_scope("s_ag0"):
        take(sums.at[0, core, held], all_recv.at[0])
        pair_all = remote(sums.at[0, core], sums.at[0, core], 6, pair_recv.at[0], 1)
        pair_all.start()
    with jax.named_scope("s_img1"):
        image = gathered(0, core)
        projected = []
        for side in range(2):
            terms = [
                mm_nt(image[:, part * width : (part + 1) * width], cells(part, side)) for part in range(n_gx)
            ]
            projected.append(sum(terms[1:], terms[0]))
        spread(1, image_of(projected))
    with jax.named_scope("s_rs1"):
        total(1)
    with jax.named_scope("s_chol0"):
        image = whole(0)
        inverse = inverse_cholesky(mm_nt(image, image))
    with jax.named_scope("s_ag1"):
        pair_copy(1, 0).start()
        for k in reversed(peers):
            take(sums.at[1, core, mine], all_recv.at[k // 2])
            pair_copy(1, k).start()
    with jax.named_scope("s_pair1"):
        image = whole(1)
    with jax.named_scope("s_chol1"):
        image = mm(inverse, image)
        inverse = inverse_cholesky(mm_nt(image, image))
        raw = None
        for part in range(n_gx):
            term = mm_nt(cells(part, 0), image[:, part * width : (part + 1) * width])
            raw = term if raw is None else raw + term
        truncated = mm_nt(raw, inverse)

    share = cells_z // n
    for s in range(species):
        for line in range(lines):
            at = (s * lines + line) * cells_z
            core_out[:, line, s * rank : (s + 1) * rank] = truncated[at : at + cells_z]

    spot = my_yz * n_gx + my_x

    def core_copy(k):
        peer = partner(k)
        return remote(core_out.at[pl.ds(peer * share, share)], core_ref.at[spot], 8, core_recv.at[0], k)

    everyone = range(n - 1, 0, -1)
    with jax.named_scope("s_a2astart"):
        for k in everyone:
            core_copy(k).start()
    with jax.named_scope("s_factor"):
        core_ref[spot] = core_out[pl.ds(me * share, share)]
        factor_ref[...] = mm(inverse, image)
    with jax.named_scope("s_drain"):
        take(xf.at[my_x, 0], send_sem.at[0])
        for side in range(2):
            take(xf.at[my_x, side], send_sem.at[1])
        for turn in range(2):
            take(parts.at[turn], send_sem.at[2 + turn])
            take(parts.at[turn], send_sem.at[4 + turn])
            take(sums.at[turn, core], send_sem.at[6 + turn])
        take(core_ref.at[pl.ds(0, n - 1)], send_sem.at[8])
    with jax.named_scope("s_a2await"):
        take(core_ref.at[pl.ds(0, n - 1)], core_recv.at[0])


def finish(core_in, factor_in, core_hbm, factor_hbm, core_buf, sem):
    lines = core_in.shape[2]
    factor_copy = pltpu.make_async_copy(factor_in, factor_hbm, sem.at[0])
    factor_copy.start()
    for spot in range(core_in.shape[0]):
        core_buf[:, spot * lines : (spot + 1) * lines] = core_in[spot]
    core_copy = pltpu.make_async_copy(core_buf, core_hbm, sem.at[1])
    core_copy.start()
    factor_copy.wait()
    core_copy.wait()


def kernel_program(tensor, start_basis, n_gx, n_yz, rows):
    n = n_gx * n_yz
    species, width, lines_held, cells_z = tensor.shape
    rank, total = start_basis.shape
    half = rank // 2
    lines = lines_held // n_gx
    cell_count = species * lines_held * n_yz * cells_z
    share = cells_z // n
    out = species * rank
    owners = n // 2
    dma = pltpu.SemaphoreType.DMA
    core, factor = pl.pallas_call(
        functools.partial(kernel, (n_gx, n_yz, cell_count)),
        out_shape=(
            pltpu.VMEM((n, share, lines, out), jnp.float32),
            pltpu.VMEM((rank, total), jnp.float32),
        ),
        in_specs=[pl.BlockSpec(memory_space=pltpu.HBM)] * 2,
        out_specs=(pl.BlockSpec(memory_space=pltpu.VMEM),) * 2,
        scratch_shapes=[
            pltpu.VMEM((n_gx, 2, species, lines, cells_z, width), jnp.float32),
            pltpu.VMEM((n_gx, half, width), jnp.float32),
            pltpu.VMEM((2, owners, rows, LANES), jnp.float32),
            pltpu.VMEM((2, owners - 1, rows, LANES), jnp.float32),
            pltpu.VMEM((2, 2, owners, rows, LANES), jnp.float32),
            pltpu.VMEM((cells_z, lines, out), jnp.float32),
            dma((2,)),
            dma((9,)),
            dma((species,)),
            dma((2,)),
            dma((2,)),
            dma((owners,)),
            dma((2,)),
            dma((1,)),
        ],
        compiler_params=pltpu.CompilerParams(collective_id=0, has_side_effects=True),
    )(tensor.transpose(0, 2, 3, 1), start_basis)
    return pl.pallas_call(
        finish,
        out_shape=(
            jax.ShapeDtypeStruct((share, n * lines, out), jnp.float32),
            jax.ShapeDtypeStruct((rank, total), jnp.float32),
        ),
        in_specs=[pl.BlockSpec(memory_space=pltpu.VMEM)] * 2,
        out_specs=(pl.BlockSpec(memory_space=pltpu.HBM),) * 2,
        scratch_shapes=[pltpu.VMEM((share, n * lines, out), jnp.float32), dma((2,))],
        compiler_params=pltpu.CompilerParams(vmem_limit_bytes=4 << 20),
    )(core, factor)


def orthonormal(image_rows):
    small_gram = jnp.dot(image_rows, image_rows.T, precision=HIGHEST)
    lower_factor = jnp.linalg.cholesky(small_gram)
    return lax.linalg.triangular_solve(lower_factor, image_rows, left_side=True, lower=True)


def collective_program(tensor, start_basis):
    regrouped = lax.all_to_all(tensor, "gx", split_axis=2, concat_axis=1, tiled=True)
    species, _, lines, cells_z = regrouped.shape
    cell_count = species * lines * lax.axis_size("gx") * lax.axis_size("yz") * cells_z
    gram_matrix = lax.dot_general(
        regrouped, regrouped, (((0, 2, 3), (0, 2, 3)), ((), ())), precision=HIGHEST
    )
    gram_matrix = lax.psum(gram_matrix, ("gx", "yz")) / cell_count
    basis = start_basis
    for _ in range(2):
        basis = orthonormal(jnp.dot(basis, gram_matrix, precision=HIGHEST))
    core_local = jnp.einsum("kx,sxyz->zysk", basis, regrouped, precision=HIGHEST)
    core_local = core_local.reshape(cells_z, lines, species * basis.shape[0])
    core_tensor = lax.all_to_all(
        lax.all_to_all(core_local, "gx", split_axis=0, concat_axis=1, tiled=True),
        "yz",
        split_axis=0,
        concat_axis=1,
        tiled=True,
    )
    return core_tensor, basis


def solution(mesh):
    n_gx, n_yz = mesh.shape["gx"], mesh.shape["yz"]
    n = n_gx * n_yz

    def local(tensor, start_basis):
        species, width, lines_held, cells_z = tensor.shape
        rank, total = start_basis.shape
        half, owners = rank // 2, n // 2
        fits = n_gx == 2 and n_yz % 2 == 0 and n & (n - 1) == 0 and rank % (2 * SUBLANES) == 0
        fits = fits and width % LANES == 0 and lines_held % n_gx == 0 and cells_z % max(n, SUBLANES) == 0
        fits = fits and species * width * lines_held * cells_z <= 1 << 19
        rows, left_over = divmod(half * (total // LANES), owners)
        if fits and left_over == 0 and rows and half % rows == 0:
            return kernel_program(tensor, start_basis, n_gx, n_yz, rows)
        return collective_program(tensor, start_basis)

    return jax.shard_map(
        local,
        mesh=mesh,
        in_specs=(P(None, "gx", "yz", None), P()),
        out_specs=(P(("gx", "yz"), None, None), P()),
        check_vma=False,
    )
```

```python
import functools

import jax
import jax.numpy as jnp
from jax import lax
from jax.experimental import pallas as pl
from jax.experimental.pallas import tpu as pltpu
from jax.sharding import PartitionSpec as P

HIGHEST = lax.Precision.HIGHEST
MESH = pl.DeviceIdType.MESH
LANES = 128
SUBLANES = 8


def mm(a, b):
    return lax.dot_general(
        a, b, (((1,), (0,)), ((), ())), precision=HIGHEST, preferred_element_type=jnp.float32
    )


def mm_nt(a, b):
    return lax.dot_general(
        a, b, (((1,), (1,)), ((), ())), precision=HIGHEST, preferred_element_type=jnp.float32
    )


def inverse_cholesky(gram, panel=2 * SUBLANES):
    rank = gram.shape[0]
    wide = -(-rank // LANES) * LANES
    row_id = lax.broadcasted_iota(jnp.int32, (SUBLANES, wide), 0)
    lane_id = lax.broadcasted_iota(jnp.int32, (SUBLANES, wide), 1)
    left = jnp.concatenate([gram, jnp.zeros((rank, wide - rank), jnp.float32)], axis=1) if wide > rank else gram
    count = rank // SUBLANES
    left = [left[i * SUBLANES : (i + 1) * SUBLANES] for i in range(count)]
    done = []
    for base in range(0, rank, panel):
        at = base // SUBLANES
        spread = [
            {
                i: jnp.broadcast_to(left[i][:, base + c : base + c + 1], (SUBLANES, wide))
                for i in range(at + c // SUBLANES, count)
            }
            for c in range(panel)
        ]
        inside = (lane_id >= base) & (lane_id < base + panel)
        for i in range(at, count):
            unit = jnp.where(row_id + i * SUBLANES == lane_id, 1.0, 0.0) if i < at + panel // SUBLANES else 0.0
            left[i] = jnp.where(inside, unit, left[i])
        for c in range(panel):
            block, row = at + c // SUBLANES, c % SUBLANES
            pivot = spread[c][block][row : row + 1]
            scale = 1.0 / pivot
            tall = jnp.broadcast_to(pivot, (SUBLANES, wide))
            pivots = tall if row == 0 else jnp.where(row_id == row, tall, pivots)
            factor = {i: spread[c][i] * scale for i in range(block, count)}
            factor[block] = jnp.where(row_id > row, factor[block], 0.0)
            for later in range(c + 1, panel):
                first, sub = at + later // SUBLANES, later % SUBLANES
                value = spread[c][first][sub : sub + 1]
                for i in range(first, count):
                    spread[later][i] = spread[later][i] - factor[i] * value
            pivot_row = left[block][row : row + 1]
            for i in range(block, count):
                left[i] = left[i] - factor[i] * pivot_row
            if row == SUBLANES - 1:
                lower = jnp.where(lane_id <= row_id + block * SUBLANES, left[block], 0.0)
                done.append(lower / jnp.sqrt(pivots))
    return jnp.concatenate(done, axis=0)[:, :rank]


def kernel(
    shape,
    x_hbm,
    start_hbm,
    core_ref,
    factor_ref,
    xa,
    xf,
    start,
    product,
    product_in,
    stage0,
    parts0,
    stage,
    parts,
    sums,
    core_out,
    news_sem,
    local_sem,
    send_sem,
    cell_recv,
    product_recv,
    sum_recv,
    all_recv,
    pair_recv,
    core_recv,
):
    n_gx, n_yz, cell_count = shape
    n = n_gx * n_yz
    my_x, my_yz = lax.axis_index("gx"), lax.axis_index("yz")
    me = my_x * n_yz + my_yz
    core = lax.rem(my_yz, 2)
    mine = lax.div(me, 2)
    other_x = 1 - my_x
    _, _, species, lines, cells_z, width = xf.shape
    half = start.shape[0]
    rank = 2 * half
    owners, rows = stage.shape[:2]
    per_column = half // rows
    held_cells = species * lines * cells_z
    flips = [1 - 2 * lax.rem(lax.div(me, 1 << bit), 2) for bit in range(n.bit_length() - 1)]
    peers = range(n - 2, 0, -2)
    near_peers = range(n_yz - 2, 0, -2)
    near_owners = n_yz // 2
    near_mine = lax.div(my_yz, 2)

    def place(flat):
        return {"gx": lax.div(flat, n_yz), "yz": lax.rem(flat, n_yz)}

    def partner(k):
        return me + sum((1 << bit) * flip for bit, flip in enumerate(flips) if k >> bit & 1)

    def remote(src, dst, send, recv, k):
        return pltpu.make_async_remote_copy(
            src_ref=src,
            dst_ref=dst,
            send_sem=send_sem.at[send],
            recv_sem=recv,
            device_id=place(partner(k)),
            device_id_type=MESH,
        )

    def take(ref, sem):
        pltpu.make_async_copy(ref, ref, sem).wait()

    barrier = pltpu.get_barrier_semaphore()
    across = n_yz
    bits = [1, across, *(1 << bit for bit in range(1, n_yz.bit_length() - 1))]
    for k in bits:
        pl.semaphore_signal(barrier, inc=1, device_id=place(partner(k)), device_id_type=MESH)

    own_copy = pltpu.make_async_copy(x_hbm, xa.at[0], local_sem.at[0])
    own_copy.start()
    mine_rows = pl.ds(pl.multiple_of(core * half, SUBLANES), half)
    mine_columns = pl.ds(pl.multiple_of(my_x * width, LANES), width)
    start_copy = pltpu.make_async_copy(start_hbm.at[mine_rows, mine_columns], start, local_sem.at[1])
    start_copy.start()
    kept = pl.ds(my_x * lines, lines)
    given = pl.ds(other_x * lines, lines)
    kept_copy = pltpu.make_async_copy(x_hbm.at[:, kept], xf.at[my_x, 0], local_sem.at[2])
    kept_copy.start()

    with jax.named_scope("s_barrier"):
        pl.semaphore_wait(barrier, len(bits))

    pair_cells = remote(x_hbm, xa.at[1], 0, cell_recv.at[0], 1)
    x_copy = remote(x_hbm.at[:, given], xf.at[my_x, 0], 1, cell_recv.at[1], across)
    relay = remote(xf.at[other_x, 0], xf.at[other_x, 1], 2, cell_recv.at[2], 1)
    pair_kept = pltpu.make_async_copy(xa.at[1, :, kept], xf.at[my_x, 1], local_sem.at[3])

    def cells(part, side):
        return xf[part, side].reshape(held_cells, width)

    def half_cells(side):
        return xa[side].reshape(n_gx * held_cells, width)

    def send_product(side):
        product[side] = mm_nt(start[...], half_cells(side)) * (1.0 / cell_count)
        remote(product.at[side], product_in.at[side], 3, product_recv.at[side], across).start()

    with jax.named_scope("s_xex"):
        pair_cells.start()
        own_copy.wait()
        start_copy.wait()
        send_product(0)
        take(xa.at[1], cell_recv.at[0])
        send_product(1)
        pair_kept.start()
    with jax.named_scope("s_news"):
        for i, k in enumerate(bits):
            pl.semaphore_signal(news_sem.at[i], inc=1, device_id=place(partner(k)), device_id_type=MESH)
            pl.semaphore_wait(news_sem.at[i], 1)
    with jax.named_scope("s_prod"):
        image = None
        for side in range(2):
            take(product_in.at[side], product_recv.at[side])
            term = mm(product[side] + product_in[side], half_cells(side))
            image = term if image is None else image + term

    def image_of(projected):
        projected = [term * (1.0 / cell_count) for term in projected]
        columns = [sum(mm(projected[side], cells(part, side)) for side in range(2)) for part in range(n_gx)]
        return jnp.concatenate(columns, axis=1)

    def near_sum_copy(k):
        block = lax.div(lax.rem(partner(k), n_yz), 2)
        return remote(stage0.at[block], parts0.at[k // 2 - 1], 4, sum_recv.at[0], k)

    def sum_copy(k):
        return remote(stage.at[lax.div(partner(k), 2)], parts.at[k // 2 - 1], 5, sum_recv.at[1], k)

    def all_copy(turn, k):
        block = sums.at[turn, core, mine]
        return remote(block, block, 6 + turn, all_recv.at[k // 2 if turn else 0], k)

    def pair_copy(turn, k):
        block = sums.at[turn, core, lax.div(partner(k), 2)]
        return remote(block, block, 9, pair_recv.at[1], 1)

    def spread(buffer, image):
        for owner in range(buffer.shape[0]):
            column, block = owner // per_column, owner % per_column
            buffer[owner] = image[block * rows : (block + 1) * rows, column * LANES : (column + 1) * LANES]

    def total(turn, terms):
        while len(terms) > 1:
            terms = [a + b for a, b in zip(terms[::2], terms[1::2])] + ([terms[-1]] if len(terms) % 2 else [])
        sums[turn, core, mine] = terms[0]
        for k in peers:
            all_copy(turn, k).start()

    def gathered(turn, side):
        blocks = [sums[turn, side, owner] for owner in range(owners)]
        columns = [jnp.concatenate(blocks[at : at + per_column], axis=0) for at in range(0, owners, per_column)]
        return jnp.concatenate(columns, axis=1)

    held = pl.ds(0, owners - 1)

    def whole(turn):
        take(sums.at[turn, 1 - core], pair_recv.at[turn])
        return jnp.concatenate([gathered(turn, side) for side in range(2)], axis=0)

    with jax.named_scope("s_img0"):
        spread(stage0, image)
        for k in near_peers:
            near_sum_copy(k).start()
        x_copy.start()
    with jax.named_scope("s_rs0"):
        take(parts0, sum_recv.at[0])
        total(0, [stage0[near_mine]] + [parts0[k // 2 - 1] for k in near_peers])
    with jax.named_scope("s_ag0"):
        take(xf.at[other_x, 0], cell_recv.at[1])
        relay.start()
        take(sums.at[0, core, held], all_recv.at[0])
        pair_all = remote(sums.at[0, core], sums.at[0, core], 8, pair_recv.at[0], 1)
        pair_all.start()
    with jax.named_scope("s_img1"):
        image = gathered(0, core)
        kept_copy.wait()
        pair_kept.wait()
        take(xf.at[other_x, 1], cell_recv.at[2])
        projected = []
        for side in range(2):
            terms = [
                mm_nt(image[:, part * width : (part + 1) * width], cells(part, side)) for part in range(n_gx)
            ]
            projected.append(sum(terms[1:], terms[0]))
        spread(stage, image_of(projected))
        for k in peers:
            sum_copy(k).start()
    with jax.named_scope("s_rs1"):
        take(parts, sum_recv.at[1])
        total(1, [stage[mine]] + [parts[k // 2 - 1] for k in peers])
    with jax.named_scope("s_chol0"):
        image = whole(0)
        inverse = inverse_cholesky(mm_nt(image, image))
    with jax.named_scope("s_ag1"):
        pair_copy(1, 0).start()
        for k in reversed(peers):
            take(sums.at[1, core, mine], all_recv.at[k // 2])
            pair_copy(1, k).start()
    with jax.named_scope("s_pair1"):
        image = whole(1)
    with jax.named_scope("s_chol1"):
        image = mm(inverse, image)
        inverse = inverse_cholesky(mm_nt(image, image))
        raw = None
        for part in range(n_gx):
            term = mm_nt(cells(part, 0), image[:, part * width : (part + 1) * width])
            raw = term if raw is None else raw + term
        truncated = mm_nt(raw, inverse)

    share = cells_z // n
    for s in range(species):
        for line in range(lines):
            at = (s * lines + line) * cells_z
            core_out[:, line, s * rank : (s + 1) * rank] = truncated[at : at + cells_z]

    spot = my_yz * n_gx + my_x

    def core_copy(k):
        peer = partner(k)
        return remote(core_out.at[pl.ds(peer * share, share)], core_ref.at[spot], 10, core_recv.at[0], k)

    everyone = range(n - 1, 0, -1)
    with jax.named_scope("s_a2astart"):
        for k in everyone:
            core_copy(k).start()
    with jax.named_scope("s_factor"):
        core_ref[spot] = core_out[pl.ds(me * share, share)]
        factor_ref[...] = mm(inverse, image)
    with jax.named_scope("s_drain"):
        take(xa.at[0], send_sem.at[0])
        take(xf.at[my_x, 0], send_sem.at[1])
        take(xf.at[other_x, 0], send_sem.at[2])
        take(product, send_sem.at[3])
        take(parts0, send_sem.at[4])
        take(parts, send_sem.at[5])
        for turn in range(2):
            take(parts, send_sem.at[6 + turn])
            take(sums.at[turn, core], send_sem.at[8 + turn])
        take(core_ref.at[pl.ds(0, n - 1)], send_sem.at[10])
    with jax.named_scope("s_a2await"):
        take(core_ref.at[pl.ds(0, n - 1)], core_recv.at[0])


def finish(core_in, factor_in, core_hbm, factor_hbm, core_buf, sem):
    lines = core_in.shape[2]
    factor_copy = pltpu.make_async_copy(factor_in, factor_hbm, sem.at[0])
    factor_copy.start()
    for spot in range(core_in.shape[0]):
        core_buf[:, spot * lines : (spot + 1) * lines] = core_in[spot]
    core_copy = pltpu.make_async_copy(core_buf, core_hbm, sem.at[1])
    core_copy.start()
    factor_copy.wait()
    core_copy.wait()


def kernel_program(tensor, start_basis, n_gx, n_yz, rows):
    n = n_gx * n_yz
    species, width, lines_held, cells_z = tensor.shape
    rank, total = start_basis.shape
    half = rank // 2
    lines = lines_held // n_gx
    cell_count = species * lines_held * n_yz * cells_z
    share = cells_z // n
    out = species * rank
    owners = n // 2
    dma = pltpu.SemaphoreType.DMA
    core, factor = pl.pallas_call(
        functools.partial(kernel, (n_gx, n_yz, cell_count)),
        out_shape=(
            pltpu.VMEM((n, share, lines, out), jnp.float32),
            pltpu.VMEM((rank, total), jnp.float32),
        ),
        in_specs=[pl.BlockSpec(memory_space=pltpu.HBM)] * 2,
        out_specs=(pl.BlockSpec(memory_space=pltpu.VMEM),) * 2,
        scratch_shapes=[
            pltpu.VMEM((2, species, lines_held, cells_z, width), jnp.float32),
            pltpu.VMEM((n_gx, 2, species, lines, cells_z, width), jnp.float32),
            pltpu.VMEM((half, width), jnp.float32),
            pltpu.VMEM((2, half, species * lines_held * cells_z), jnp.float32),
            pltpu.VMEM((2, half, species * lines_held * cells_z), jnp.float32),
            pltpu.VMEM((n_yz // 2, rows, LANES), jnp.float32),
            pltpu.VMEM((n_yz // 2 - 1, rows, LANES), jnp.float32),
            pltpu.VMEM((owners, rows, LANES), jnp.float32),
            pltpu.VMEM((owners - 1, rows, LANES), jnp.float32),
            pltpu.VMEM((2, 2, owners, rows, LANES), jnp.float32),
            pltpu.VMEM((cells_z, lines, out), jnp.float32),
            pltpu.SemaphoreType.REGULAR((n.bit_length() - 1,)),
            dma((4,)),
            dma((11,)),
            dma((3,)),
            dma((2,)),
            dma((2,)),
            dma((owners,)),
            dma((2,)),
            dma((1,)),
        ],
        compiler_params=pltpu.CompilerParams(collective_id=0, has_side_effects=True),
    )(tensor.transpose(0, 2, 3, 1), start_basis)
    return pl.pallas_call(
        finish,
        out_shape=(
            jax.ShapeDtypeStruct((share, n * lines, out), jnp.float32),
            jax.ShapeDtypeStruct((rank, total), jnp.float32),
        ),
        in_specs=[pl.BlockSpec(memory_space=pltpu.VMEM)] * 2,
        out_specs=(pl.BlockSpec(memory_space=pltpu.HBM),) * 2,
        scratch_shapes=[pltpu.VMEM((share, n * lines, out), jnp.float32), dma((2,))],
        compiler_params=pltpu.CompilerParams(vmem_limit_bytes=4 << 20),
    )(core, factor)


def orthonormal(image_rows):
    small_gram = jnp.dot(image_rows, image_rows.T, precision=HIGHEST)
    lower_factor = jnp.linalg.cholesky(small_gram)
    return lax.linalg.triangular_solve(lower_factor, image_rows, left_side=True, lower=True)


def collective_program(tensor, start_basis):
    regrouped = lax.all_to_all(tensor, "gx", split_axis=2, concat_axis=1, tiled=True)
    species, _, lines, cells_z = regrouped.shape
    cell_count = species * lines * lax.axis_size("gx") * lax.axis_size("yz") * cells_z
    gram_matrix = lax.dot_general(
        regrouped, regrouped, (((0, 2, 3), (0, 2, 3)), ((), ())), precision=HIGHEST
    )
    gram_matrix = lax.psum(gram_matrix, ("gx", "yz")) / cell_count
    basis = start_basis
    for _ in range(2):
        basis = orthonormal(jnp.dot(basis, gram_matrix, precision=HIGHEST))
    core_local = jnp.einsum("kx,sxyz->zysk", basis, regrouped, precision=HIGHEST)
    core_local = core_local.reshape(cells_z, lines, species * basis.shape[0])
    core_tensor = lax.all_to_all(
        lax.all_to_all(core_local, "gx", split_axis=0, concat_axis=1, tiled=True),
        "yz",
        split_axis=0,
        concat_axis=1,
        tiled=True,
    )
    return core_tensor, basis


def solution(mesh):
    n_gx, n_yz = mesh.shape["gx"], mesh.shape["yz"]
    n = n_gx * n_yz

    def local(tensor, start_basis):
        species, width, lines_held, cells_z = tensor.shape
        rank, total = start_basis.shape
        half, owners = rank // 2, n // 2
        fits = n_gx == 2 and n_yz % 2 == 0 and n & (n - 1) == 0 and rank % (2 * SUBLANES) == 0
        fits = fits and width % LANES == 0 and lines_held % n_gx == 0 and cells_z % max(n, SUBLANES) == 0
        fits = fits and species * width * lines_held * cells_z <= 1 << 19
        rows, left_over = divmod(half * (total // LANES), owners)
        if fits and left_over == 0 and rows and half % rows == 0:
            return kernel_program(tensor, start_basis, n_gx, n_yz, rows)
        return collective_program(tensor, start_basis)

    return jax.shard_map(
        local,
        mesh=mesh,
        in_specs=(P(None, "gx", "yz", None), P()),
        out_specs=(P(("gx", "yz"), None, None), P()),
        check_vma=False,
    )
```
